32 devices in a mesh: parts: 2 (over y), expert: 4 (over z), tensor: 4 (over x, core).
Axes of the slice: x: 2, y: 2, z: 4, core: 2. Of those that a mesh axis runs over, the one named last changes fastest.
Arguments:
- mamba_input: bfloat16 [128, 4096], P(('parts', 'expert'), 'tensor'), parts along dimension 0, may hold values from -5 to 5
- mamba_gate: bfloat16 [128, 4096], P(('parts', 'expert'), 'tensor'), parts along dimension 0, may hold values from -5 to 5
- conv_state: bfloat16 [128, 3, 4096], P(('parts', 'expert'), None, 'tensor'), parts along dimension 0, may hold values from -5 to 5
- scan_state: float32 [128, 16, 4096], P(('parts', 'expert'), None, 'tensor'), parts along dimension 0, may hold values from -6 to 6
- conv_weight: float32 [4, 4096], P(None, 'tensor'), may hold values from -3 to 3
- conv_bias: float32 [4096], P('tensor'), may hold values from -0.5 to 0.5
- state_proj: bfloat16 [288, 4096], P(None, 'tensor'), may hold values from -0.09375 to 0.09375
- step_proj: bfloat16 [256, 4096], P(None, 'tensor'), may hold values from -0.375 to 0.375
- step_bias: float32 [4096], P('tensor'), may hold values from -4.5 to -1
- decay_log: float32 [16, 4096], P(None, 'tensor'), may hold values from 0 to 2.8
- skip_gain: float32 [4096], P('tensor'), may hold values from 0.5 to 2
- queries: bfloat16 [128, 32, 128], P(('parts', 'expert'), 'tensor'), parts along dimension 0, may hold values from -48 to 48
- new_entry: bfloat16 [128, 8, 256], P(('parts', 'expert'), 'tensor'), parts along dimension 0, may hold values from -4 to 4
- past_entries: bfloat16 [128, 8, 128, 256], P(('parts', 'expert'), 'tensor'), parts along dimension 0, may hold values from -4 to 4
- lengths: int32 [128], P(('parts', 'expert')), parts along dimension 0, may hold values from 2 to 128, as said below
- expert_input: bfloat16 [128, 2048], P(('parts', 'expert'), 'tensor'), parts along dimension 0, may hold values from -5 to 5
- routes: int32 [128, 2], P(('parts', 'expert')), parts along dimension 0, may hold values from 0 to 7, as said below
- slots: int32 [128, 2], P(('parts', 'expert')), parts along dimension 0, may hold values from 0 to 7, as said below
- gates: float32 [128, 2], P(('parts', 'expert')), parts along dimension 0, may hold values from 0.1 to 1
- inner_weights: bfloat16 [8, 2, 8192, 2048], P('expert', None, 'tensor'), may hold values from -0.125 to 0.125
- outer_weights: bfloat16 [8, 8192, 2048], P('expert', 'tensor'), may hold values from -0.09375 to 0.09375
Outputs:
- mamba_out: bfloat16 [128, 4096], P(('parts', 'expert'), 'tensor'), parts along dimension 0
- next_state: float32 [128, 16, 4096], P(('parts', 'expert'), None, 'tensor'), parts along dimension 0
- attention_out: bfloat16 [128, 4096], P(('parts', 'expert'), 'tensor'), parts along dimension 0
- expert_out: bfloat16 [128, 2048], P(('parts', 'expert'), 'tensor'), parts along dimension 0
The draws below stay inside these ranges and needn't reach their ends.
There are 2 independent parts, one for each index of `parts`. The reference program is written for one: setup_inputs(seed, part) draws one part's arguments, and reference() takes and returns one part's arrays. A program takes and returns all parts, laid end to end along the dimension named above; an argument that names none is the same for every part. Nothing has to cross between parts.
Inputs may be any that keep to these rules, and one draw needn't show every extreme that they name: `routes`: A row names 2 different experts. Within the 16 rows of one device (aligned blocks) no expert is named more than 8 times, and one expert, the same in all blocks, is named exactly 8 times in every block. slots[t, k] numbers the rows of t's block that name expert routes[t, k]: within a block the slots of one expert are distinct. `lengths`: every block of 16 sequences holds one of length 128.
All inputs are finite; a program needn't handle non-finite values.
Results may differ from the reference program's by a relative error of at most 0.006.
Values may be sent and summed in bfloat16 or wider, within the bound.
A program may use at most 128 MiB of HBM per device.

```python
import jax
import jax.numpy as jnp
from jax import lax

D = 2048
FF = 8192
EXPERTS = 8
TOP = 2
INNER = 4096
NS = 16
R = 256
CONV = 4
QH = 32
KVH = 8
HD = 128
B_DEV = 16
CACHE = 128
SEQS = 64
REP = 1
ROWS = 8
FFR = 8192
CAP = 8
PROJ = 288


def route_table(key):
    blocks = SEQS // B_DEV
    capacity = max(2, 4 * B_DEV // EXPERTS)
    hot_expert = jax.random.randint(jax.random.fold_in(key, 11), (), 0, EXPERTS).astype(jnp.int32)
    cell_count = (EXPERTS - 1) * capacity

    def one_block(block_key):
        first_key, second_key = jax.random.split(block_key)
        ranked = jax.random.permutation(first_key, cell_count)
        taken_cells = (ranked < 2 * B_DEV - capacity).astype(jnp.int32)
        counts = jnp.concatenate([jnp.full((1,), capacity, jnp.int32), jnp.sum(taken_cells.reshape(EXPERTS - 1, capacity), axis=1)])
        others = jnp.arange(EXPERTS - 1, dtype=jnp.int32)
        others = others + (others >= hot_expert).astype(jnp.int32)
        expert_order = jnp.concatenate([hot_expert[None], others])
        upper_edge = jnp.cumsum(counts)
        lower_edge = upper_edge - counts
        positions = jnp.arange(2 * B_DEV, dtype=jnp.int32)
        run_index = jnp.sum((upper_edge[None, :] <= positions[:, None]).astype(jnp.int32), axis=1)
        chosen = expert_order[run_index]
        slot_pos = positions - lower_edge[run_index]
        pair_experts = jnp.stack([chosen[:B_DEV], chosen[B_DEV:]], axis=1)
        pair_slots = jnp.stack([slot_pos[:B_DEV], slot_pos[B_DEV:]], axis=1)
        shuffle = jax.random.permutation(second_key, B_DEV)
        return (pair_experts[shuffle], pair_slots[shuffle])
    block_keys = jax.random.split(jax.random.fold_in(key, 12), blocks)
    experts_drawn, slots_drawn = jax.vmap(one_block)(block_keys)
    return (experts_drawn.reshape(SEQS, 2).astype(jnp.int32), slots_drawn.reshape(SEQS, 2).astype(jnp.int32))


def draw_routes(key, part):
    return route_table(key)[0]


def draw_slots(key, part):
    return route_table(key)[1]


def draw_lengths(key, part):
    base_len = jax.random.randint(jax.random.fold_in(key, 21), (SEQS,), 2, CACHE + 1)
    full_pick = jax.random.randint(jax.random.fold_in(key, 22), (SEQS // B_DEV,), 0, B_DEV)
    full_mask = (jnp.arange(B_DEV, dtype=jnp.int32)[None, :] == full_pick[:, None]).reshape(SEQS)
    return jnp.where(full_mask, CACHE, base_len).astype(jnp.int32)


def attention_tables(key):
    cache_shape = (SEQS, KVH, CACHE, 2 * HD)
    entries = jnp.clip(jax.random.normal(jax.random.fold_in(key, 31), cache_shape, jnp.float32), -4.0, 4.0)
    query_rows = jnp.clip(jax.random.normal(jax.random.fold_in(key, 32), (SEQS, QH, HD), jnp.float32), -4.0, 4.0)
    return (query_rows, entries)


def draw_queries(key, part):
    return attention_tables(key)[0].astype(jnp.bfloat16)


def draw_past_entries(key, part):
    return attention_tables(key)[1].astype(jnp.bfloat16)


def strengthened(drawn, rng, source, target, shards_of, factor):
    owner, partner = [(jnp.arange(drawn.shape[axis_at]) // (drawn.shape[axis_at] // shards_of)).reshape([-1 if axis == axis_at else 1 for axis in range(drawn.ndim)]) for axis_at in (source, target)]
    chosen = jax.random.permutation(rng, shards_of)[partner]
    strong = (owner == chosen) | (owner == (partner + shards_of // 2) % shards_of)
    return jnp.where(strong, factor * drawn, drawn)


def shard_levels(stream_key, extent, cuts, least, top_value):
    gain = 1.0
    for dim, parts in cuts:
        draws = jax.random.uniform(jax.random.fold_in(jax.random.fold_in(stream_key, 6), dim), (parts,), jnp.float32, least / len(cuts), top_value / len(cuts))
        gain = gain * jnp.repeat(jnp.exp(draws), extent[dim] // parts).reshape((-1,) + (1,) * (len(extent) - 1 - dim))
    return gain


def normal_values(key, extent, spread, limit, cuts=(), kind=jnp.bfloat16):
    drawn = jax.random.normal(key, extent, jnp.float32) * spread
    if len(cuts) > 0:
        drawn = shard_levels(key, extent, cuts, -0.22, 0.18) * drawn
    return jnp.clip(drawn, min=-limit, max=limit).astype(kind)


def gaussian_with(stream_key, dims, width, most, cuts, heavy, held_as=jnp.bfloat16):
    drawn = width * jax.random.normal(stream_key, dims, jnp.float32)
    if cuts:
        drawn = drawn * shard_levels(stream_key, dims, cuts, -0.22, 0.18)
    return jnp.clip(strengthened(drawn, jax.random.fold_in(stream_key, 3), *heavy), -most, most).astype(held_as)


def setup_inputs(seed: int = 0, part: int = 0) -> dict:
    splits = jax.random.split(jax.random.key(seed), 22)
    part_splits = jax.random.split(jax.random.fold_in(splits[21], part), 22)
    mamba_input = normal_values(part_splits[0], (SEQS, INNER), 1.0, 5.0, ((0, 4), (1, 4)))
    mamba_gate = normal_values(part_splits[1], (SEQS, INNER), 1.0, 5.0, ((0, 4), (1, 4)))
    conv_state = normal_values(part_splits[2], (SEQS, CONV - 1, INNER), 1.0, 5.0, ((0, 4), (2, 4)))
    scan_state = normal_values(part_splits[3], (SEQS, NS, INNER), 1.0, 6.0, ((0, 4), (2, 4)), jnp.float32)
    conv_weight = normal_values(splits[4], (CONV, INNER), CONV ** -0.5, 3.0, ((1, 4),), jnp.float32)
    conv_bias = jnp.clip(jax.random.uniform(splits[5], (INNER,), jnp.float32, -0.5, 0.5) * shard_levels(splits[5], (INNER,), ((0, 4),), -0.4, 0.0), -0.5, 0.5)
    state_proj = normal_values(splits[6], (PROJ, INNER), INNER ** -0.5, 0.09375, ((1, 4),))
    step_proj = normal_values(splits[7], (R, INNER), R ** -0.5, 0.375, ((1, 4),))
    step_bias = jnp.clip(-4.5 + 3.5 * jax.random.uniform(splits[8], (INNER,), jnp.float32) ** shard_levels(splits[8], (INNER,), ((0, 4),), -0.2, 0.2), -4.5, -1.0)
    decay_log = jnp.clip(2.8 * jax.random.uniform(splits[9], (NS, INNER), jnp.float32) ** shard_levels(splits[9], (NS, INNER), ((1, 4),), -0.2, 0.2), 0.0, 2.8)
    skip_gain = jnp.clip(0.5 + 1.5 * jax.random.uniform(splits[10], (INNER,), jnp.float32) ** shard_levels(splits[10], (INNER,), ((0, 4),), -0.2, 0.2), 0.5, 2.0)
    queries = draw_queries(jax.random.fold_in(jax.random.fold_in(splits[21], part), 71), part)
    new_entry = normal_values(part_splits[12], (SEQS, KVH, 2 * HD), 1.0, 4.0, ((0, 4), (1, 4)))
    past_entries = draw_past_entries(jax.random.fold_in(jax.random.fold_in(splits[21], part), 71), part)
    lengths = draw_lengths(jax.random.fold_in(jax.random.fold_in(splits[21], part), 71), part)
    expert_input = normal_values(part_splits[15], (SEQS, D), 1.0, 5.0, ((0, 4), (1, 4)))
    routes = draw_routes(jax.random.fold_in(jax.random.fold_in(splits[21], part), 71), part)
    slots = draw_slots(jax.random.fold_in(jax.random.fold_in(splits[21], part), 71), part)
    gates = jnp.clip(0.1 + 0.9 * jax.random.uniform(part_splits[18], (SEQS, TOP), jnp.float32) ** shard_levels(part_splits[18], (SEQS, TOP), ((0, 4),), -0.2, 0.2), 0.1, 1.0)
    inner_weights = normal_values(splits[19], (ROWS, 2, FFR, D), D ** -0.5, 0.125, ((0, 4), (2, 4)))
    outer_weights = gaussian_with(splits[20], (ROWS, FFR, D), FF ** -0.5, 0.09375, ((0, 4), (1, 4)), (1, 2, 4, 2.0))
    return dict(mamba_input=mamba_input, mamba_gate=mamba_gate, conv_state=conv_state, scan_state=scan_state, conv_weight=conv_weight, conv_bias=conv_bias, state_proj=state_proj, step_proj=step_proj, step_bias=step_bias, decay_log=decay_log, skip_gain=skip_gain, queries=queries, new_entry=new_entry, past_entries=past_entries, lengths=lengths, expert_input=expert_input, routes=routes, slots=slots, gates=gates, inner_weights=inner_weights, outer_weights=outer_weights)


def mamba_step(mamba_input, mamba_gate, conv_state, scan_state, conv_weight, conv_bias, state_proj, step_proj, step_bias, decay_log, skip_gain):
    window = jnp.concatenate([conv_state.astype(jnp.float32), mamba_input.astype(jnp.float32)[:, None, :]], axis=1)
    conv_act = jax.nn.silu(jnp.sum(window * conv_weight[None], axis=1) + conv_bias)
    mixing = lax.dot_general(conv_act.astype(jnp.bfloat16), state_proj, (((1,), (1,)), ((), ())), preferred_element_type=jnp.float32)
    low_rank = step_proj.shape[0]
    states = decay_log.shape[0]
    step_size = jax.nn.softplus(jnp.dot(mixing[:, :low_rank].astype(jnp.bfloat16), step_proj, preferred_element_type=jnp.float32) + step_bias)
    in_coef = mixing[:, low_rank:low_rank + states]
    out_coef = mixing[:, low_rank + states:]
    decay_rate = jnp.exp(-step_size[:, None, :] * jnp.exp(decay_log)[None])
    next_state = decay_rate * scan_state + (step_size * conv_act)[:, None, :] * in_coef[:, :, None]
    mixed_out = jnp.sum(next_state * out_coef[:, :, None], axis=1) + skip_gain * conv_act
    return (mixed_out * jax.nn.silu(mamba_gate.astype(jnp.float32))).astype(jnp.bfloat16), next_state


def attend(queries, new_entry, past_entries, lengths):
    seq_count, head_count, head_size = queries.shape
    groups = past_entries.shape[1]
    per_group = head_count // groups
    positions = past_entries.shape[2]
    scaling = head_size ** -0.5
    query_rows = queries.astype(jnp.float32).reshape(seq_count, groups, per_group, head_size)
    cache_keys = past_entries[..., :head_size].astype(jnp.float32)
    cache_values = past_entries[..., head_size:].astype(jnp.float32)
    scores = jnp.einsum("sgqd,sgld->sgql", query_rows, cache_keys) * scaling
    own_score = jnp.einsum("sgqd,sgd->sgq", query_rows, new_entry[..., :head_size].astype(jnp.float32)) * scaling
    live_mask = jnp.arange(positions, dtype=jnp.int32)[None, :] < lengths[:, None]
    scores = jnp.where(live_mask[:, None, None, :], scores, -jnp.inf)
    highest = jnp.maximum(jnp.max(scores, axis=3), own_score)
    weights = jnp.exp(scores - highest[..., None])
    own_weight = jnp.exp(own_score - highest)
    denominator = jnp.sum(weights, axis=3) + own_weight
    weights_low = (weights / denominator[..., None]).astype(jnp.bfloat16)
    own_low = (own_weight / denominator).astype(jnp.bfloat16)
    mixed_out = jnp.einsum("sgql,sgld->sgqd", weights_low.astype(jnp.float32), cache_values)
    mixed_out = mixed_out + own_low.astype(jnp.float32)[..., None] * new_entry[..., head_size:].astype(jnp.float32)[:, :, None, :]
    return mixed_out.reshape(seq_count, head_count * head_size).astype(jnp.bfloat16)


def expert_layer(expert_input, routes, slots, gates, inner_weights, outer_weights):
    blocks = SEQS // B_DEV
    source = jnp.broadcast_to((jnp.arange(SEQS, dtype=jnp.int32) // B_DEV)[:, None], routes.shape)
    buffer = jnp.zeros((EXPERTS, blocks, CAP, D), jnp.bfloat16)
    buffer = buffer.at[routes, source, slots].set(jnp.broadcast_to(expert_input[:, None, :], (SEQS, TOP, D)))

    def one_expert(operands):
        token_rows, inner_w, outer_w = operands
        gate_w = inner_w[:, 0].reshape(FF, D)
        up_w = inner_w[:, 1].reshape(FF, D)
        gate_val = lax.dot_general(token_rows, gate_w, (((1,), (1,)), ((), ())), preferred_element_type=jnp.float32)
        up_val = lax.dot_general(token_rows, up_w, (((1,), (1,)), ((), ())), preferred_element_type=jnp.float32)
        hidden = (jax.nn.silu(gate_val) * up_val).astype(jnp.bfloat16)
        return jnp.dot(hidden, outer_w.reshape(FF, D), preferred_element_type=jnp.float32)

    results = lax.map(one_expert, (buffer.reshape(EXPERTS, blocks * CAP, D), inner_weights.reshape(EXPERTS, REP, 2, FFR, D), outer_weights.reshape(EXPERTS, REP, FFR, D)))
    results = results.reshape(EXPERTS, blocks, CAP, D)
    picked = results[routes, source, slots]
    return jnp.sum(gates[:, :, None] * picked, axis=1).astype(jnp.bfloat16)


def reference(mamba_input, mamba_gate, conv_state, scan_state, conv_weight, conv_bias, state_proj, step_proj, step_bias, decay_log, skip_gain, queries, new_entry, past_entries, lengths, expert_input, routes, slots, gates, inner_weights, outer_weights):
    mamba_out, next_state = mamba_step(mamba_input, mamba_gate, conv_state, scan_state, conv_weight, conv_bias, state_proj, step_proj, step_bias, decay_log, skip_gain)
    attention_out = attend(queries, new_entry, past_entries, lengths)
    expert_out = expert_layer(expert_input, routes, slots, gates, inner_weights, outer_weights)
    return (mamba_out, next_state, attention_out, expert_out)
```

```python
import functools

import jax
import jax.numpy as jnp
from jax import lax
from jax.experimental import pallas as pl
from jax.experimental.pallas import tpu as pltpu
from jax.sharding import PartitionSpec as P

EXPERTS = 8
MESH = pl.DeviceIdType.MESH
F32 = jnp.float32
BF16 = jnp.bfloat16
EXACT = lax.Precision.HIGHEST
NT = (((1,), (1,)), ((), ()))
NN = (((1,), (0,)), ((), ()))


def dot(a, b, dims):
    return lax.dot_general(a, b, dims, preferred_element_type=F32)


def eye(n):
    rows = lax.broadcasted_iota(jnp.int32, (n, n), 0)
    cols = lax.broadcasted_iota(jnp.int32, (n, n), 1)
    return jnp.where(rows == cols, 1.0, 0.0).astype(F32)


def kernel(
    E,
    T,
    fc,
    mi_h, mg_h, cs_h, ss_h, cw_h, cb_h, sp_h, tp_h, sb_h, dl_h, sg_h,
    q_h, ne_h, pe_h, len_h, xi_h, ro_h, ga_h, iw_h, ow_h,
    mo_h, ns_h, ao_h, eo_h,
    mi, mg, cs, ss, cw, cb, sp, tp, sb, dl, sg, q, ne, pe, lens, ro, ga, iw, ow,
    X, wr, mixp, mixr, conv, yv, stv, scuv, score, knew, vnew, ao, mo, hid, psend, rrecv, tot, tsend, erecv, eo,
    in_sem, pe_sem, iw_sem, ow_sem, out_sem, x_sem,
    as_sem, ar_sem, ws_sem, wr_sem, bs_sem, br_sem, ms_sem, mr_sem, rs_sem, rr_sem, es_sem, er_sem,
):
    me = lax.axis_index("expert")
    mt = lax.axis_index("tensor")
    B, Dl = xi_h.shape
    L, _, F, D = iw_h.shape
    S, H, HD = q_h.shape
    G = ne_h.shape[1]
    per = H // G
    N = dl_h.shape[0]
    R = tp_h.shape[0]
    reps = max(1, E // EXPERTS)
    nf = F // fc
    remote = functools.partial(pltpu.make_async_remote_copy, device_id_type=MESH)

    def epeer(d):
        return lax.rem(me + d, E)

    def tpeer(d):
        return lax.rem(mt + d, T)

    barrier = pltpu.get_barrier_semaphore()
    for d in range(1, E):
        pl.semaphore_signal(barrier, inc=1, device_id={"expert": epeer(d)}, device_id_type=MESH)
    for d in range(1, T):
        pl.semaphore_signal(barrier, inc=1, device_id={"tensor": tpeer(d)}, device_id_type=MESH)

    pairs = [
        (ro_h, ro), (ga_h, ga), (len_h, lens), (cs_h, cs), (mi_h, mi), (cw_h, cw), (cb_h, cb), (sp_h, sp),
        (q_h, q), (ne_h, ne), (tp_h, tp), (sb_h, sb), (dl_h, dl), (sg_h, sg), (mg_h, mg), (ss_h, ss),
    ]
    local = {}
    for n, (src, dst) in enumerate(pairs):
        local[id(dst)] = pltpu.make_async_copy(src, dst, in_sem.at[n])

    def block(e, t):
        return X.at[pl.ds(pl.multiple_of(e * B, B), B), pl.ds(pl.multiple_of(t * Dl, Dl), Dl)]

    def rows(ref, e):
        return ref.at[pl.ds(pl.multiple_of(e * B, B), B)]

    own_x = pltpu.make_async_copy(xi_h, block(me, mt), x_sem)
    early = [ro, ga, lens, cs, mi, cw, cb, sp, q, ne]
    late = [tp, sb, dl, sg, mg, ss]
    for dst in early:
        local[id(dst)].start()
    own_x.start()
    pcopy = pltpu.make_async_copy(pe_h, pe, pe_sem)
    pcopy.start()
    for dst in late:
        local[id(dst)].start()

    def inner_copy(l, i):
        at = pl.ds(pl.multiple_of(i * fc, fc), fc)
        return pltpu.make_async_copy(iw_h.at[l, :, at, :], iw.at[l, :, at, :], iw_sem.at[l, i])

    for l in range(L):
        @pl.loop(0, nf)
        def _(i, l=l):
            inner_copy(l, i).start()

    def outer_copy(j, l):
        cols = pl.ds(pl.multiple_of(tpeer(j + 1) * Dl, Dl), Dl)
        return pltpu.make_async_copy(ow_h.at[l, :, cols], ow.at[j, pl.ds(l * F, F), :], ow_sem.at[j, l])

    for j in range(T):
        for l in range(L):
            outer_copy(j, l).start()

    local[id(ro)].wait()
    local[id(ga)].wait()
    width = wr.shape[1]
    table = jnp.zeros((width, B), F32)
    row_of = lax.broadcasted_iota(jnp.int32, (width, B), 0)
    for k in range(ro.shape[0]):
        first = ro[k : k + 1, :] * reps
        table = table + jnp.where((row_of >= first) & (row_of < first + reps), ga[k : k + 1, :], 0.0)
    table = lax.dot_general(eye(B), table, NT, precision=EXACT, preferred_element_type=F32)
    wr[pl.ds(pl.multiple_of(me * B, B), B), :] = table

    pl.semaphore_wait(barrier, E - 1 + T - 1)

    def send_a(d):
        p = epeer(d)
        return remote(src_ref=xi_h, dst_ref=block(me, mt), send_sem=as_sem.at[p], recv_sem=ar_sem.at[me],
                      device_id={"expert": p})

    def recv_a(e):
        return remote(src_ref=xi_h, dst_ref=block(e, mt), send_sem=as_sem.at[e], recv_sem=ar_sem.at[e],
                      device_id={"expert": e})

    def send_w(d):
        p = epeer(d)
        return remote(src_ref=rows(wr, me), dst_ref=rows(wr, me), send_sem=ws_sem.at[p], recv_sem=wr_sem.at[me],
                      device_id={"expert": p})

    def recv_w(e):
        return remote(src_ref=rows(wr, e), dst_ref=rows(wr, e), send_sem=ws_sem.at[e], recv_sem=wr_sem.at[e],
                      device_id={"expert": e})

    def send_b(e, d, own):
        p = tpeer(d)
        return remote(src_ref=xi_h if own else block(e, mt), dst_ref=block(e, mt), send_sem=bs_sem.at[e, p],
                      recv_sem=br_sem.at[e, mt], device_id={"tensor": p})

    def recv_b(e, t):
        return remote(src_ref=xi_h, dst_ref=block(e, t), send_sem=bs_sem.at[e, t], recv_sem=br_sem.at[e, t],
                      device_id={"tensor": t})

    for d in range(1, E):
        send_a(d).start()
    for d in range(1, T):
        send_b(me, d, True).start()
    for d in range(1, E):
        send_w(d).start()

    for ref in (cs, mi, cw, cb, sp):
        local[id(ref)].wait()
    taps = cw.shape[0]
    pre = mi[...].astype(F32) * cw[taps - 1 : taps, :]
    for k in range(taps - 1):
        pre = pre + cs[k].astype(F32) * cw[k : k + 1, :]
    act = jax.nn.silu(pre + cb[...])
    conv[...] = act
    mixp[...] = dot(act.astype(BF16), sp[...], NT)

    def send_m(d):
        p = tpeer(d)
        return remote(src_ref=mixp, dst_ref=mixr.at[mt], send_sem=ms_sem.at[p], recv_sem=mr_sem.at[mt],
                      device_id={"tensor": p})

    def recv_m(t):
        return remote(src_ref=mixp, dst_ref=mixr.at[t], send_sem=ms_sem.at[t], recv_sem=mr_sem.at[t],
                      device_id={"tensor": t})

    for d in range(1, T):
        send_m(d).start()

    for ref in (lens, q, ne):
        local[id(ref)].wait()
    pcopy.wait()
    head_row = lax.broadcasted_iota(jnp.int32, (H, HD), 0)
    places = lax.broadcasted_iota(jnp.int32, (H, pe.shape[2]), 1)
    place_row = lax.broadcasted_iota(jnp.int32, (H, pe.shape[2]), 0)

    def by_group(parts, row):
        out = parts[0]
        for g in range(1, G):
            out = jnp.where(row >= g * per, parts[g], out)
        return out

    for s in range(S):
        qs = q[s]
        sc = by_group([dot(qs, pe[s, g, :, :HD], NT) for g in range(G)], place_row)
        score[s] = jnp.where(places < lens[s], sc, -jnp.inf)
        entry = ne[s].astype(F32)
        knew[s] = by_group([jnp.broadcast_to(entry[g : g + 1, :HD], (H, HD)) for g in range(G)], head_row)
        vnew[s] = by_group([jnp.broadcast_to(entry[g : g + 1, HD:], (H, HD)) for g in range(G)], head_row)

    for d in range(1, E):
        e = epeer(d)
        recv_a(e).wait_recv()
        for k in range(1, T):
            send_b(e, k, False).start()

    scaling = HD ** (-0.5)
    sc = score[...] * scaling
    own_score = jnp.sum(q[...].astype(F32) * knew[...], axis=2, keepdims=True) * scaling
    highest = jnp.maximum(jnp.max(sc, axis=2, keepdims=True), own_score)
    weights = jnp.exp(sc - highest)
    own_weight = jnp.exp(own_score - highest)
    total = jnp.sum(weights, axis=2, keepdims=True) + own_weight
    score[...] = weights / total
    vnew[...] = (own_weight / total).astype(BF16).astype(F32) * vnew[...]
    for s in range(S):
        low = score[s].astype(BF16)
        mixed = by_group([dot(low, pe[s, g, :, HD:], NN) for g in range(G)], head_row)
        knew[s] = mixed + vnew[s]
    for h in range(H):
        ao[:, h * HD : (h + 1) * HD] = knew[:, h, :].astype(BF16)
    out_a = pltpu.make_async_copy(ao, ao_h, out_sem.at[0])
    out_a.start()

    for ref in (tp, sb, dl, sg, mg, ss):
        local[id(ref)].wait()
    mixing = mixp[...]
    for d in range(1, T):
        t = tpeer(d)
        recv_m(t).wait_recv()
        mixing = mixing + mixr[t]
    step = jax.nn.softplus(dot(mixing[:, :R].astype(BF16), tp[...], NN) + sb[...])
    stv[...] = step
    scuv[...] = step * conv[...]
    coef = lax.dot_general(mixing[:, R:], eye(S), (((0,), (0,)), ((), ())), precision=EXACT, preferred_element_type=F32)
    decay = jnp.exp(dl[...])
    for s in range(S):
        nxt = jnp.exp(-stv[s : s + 1, :] * decay) * ss[s] + scuv[s : s + 1, :] * coef[:N, s : s + 1]
        ss[s] = nxt
        yv[s : s + 1, :] = jnp.sum(nxt * coef[N:, s : s + 1], axis=0, keepdims=True)
    out_s = pltpu.make_async_copy(ss, ns_h, out_sem.at[1])
    out_s.start()
    mo[...] = ((yv[...] + sg[...] * conv[...]) * jax.nn.silu(mg[...].astype(F32))).astype(BF16)
    out_m = pltpu.make_async_copy(mo, mo_h, out_sem.at[2])
    out_m.start()

    own_x.wait()
    for d in range(1, E):
        recv_w(epeer(d)).wait_recv()
    for e in range(E):
        for d in range(1, T):
            recv_b(lax.rem(me + e, E), tpeer(d)).wait_recv()
    lanes = lax.broadcasted_iota(jnp.int32, wr.shape, 1)
    for l in range(L):
        weight = jnp.sum(jnp.where(lanes == me * L + l, wr[...], 0.0), axis=1, keepdims=True)

        @pl.loop(0, nf)
        def _(i, l=l, weight=weight):
            inner_copy(l, i).wait()
            at = pl.ds(pl.multiple_of(i * fc, fc), fc)
            x = X[...]
            gate = dot(x, iw[l, 0, at, :], NT)
            up = dot(x, iw[l, 1, at, :], NT)
            to = pl.ds(pl.multiple_of(l * F + i * fc, fc), fc)
            hid[:, to] = (jax.nn.silu(gate) * up * weight).astype(BF16)

    def send_r(j):
        p = tpeer(j + 1)
        return remote(src_ref=psend.at[j], dst_ref=rrecv.at[mt], send_sem=rs_sem.at[j], recv_sem=rr_sem.at[mt],
                      device_id={"tensor": p})

    def recv_r(t):
        return remote(src_ref=psend.at[0], dst_ref=rrecv.at[t], send_sem=rs_sem.at[0], recv_sem=rr_sem.at[t],
                      device_id={"tensor": t})

    for j in range(T):
        for l in range(L):
            outer_copy(j, l).wait()
        part = dot(hid[...], ow[j], NN)
        if j < T - 1:
            psend[j] = part.astype(BF16)
            send_r(j).start()
    for d in range(1, T):
        t = tpeer(d)
        recv_r(t).wait_recv()
        part = part + rrecv[t].astype(F32)
    tot[...] = part
    tsend[...] = part.astype(BF16)

    def send_e(d):
        p = epeer(d)
        return remote(src_ref=rows(tsend, p), dst_ref=erecv.at[me], send_sem=es_sem.at[p], recv_sem=er_sem.at[me],
                      device_id={"expert": p})

    def recv_e(e):
        return remote(src_ref=rows(tsend, e), dst_ref=erecv.at[e], send_sem=es_sem.at[e], recv_sem=er_sem.at[e],
                      device_id={"expert": e})

    for d in range(1, E):
        send_e(d).start()
    final = tot[pl.ds(pl.multiple_of(me * B, B), B), :]
    for d in range(1, E):
        e = epeer(d)
        recv_e(e).wait_recv()
        final = final + erecv[e].astype(F32)
    eo[...] = final.astype(BF16)
    out_e = pltpu.make_async_copy(eo, eo_h, out_sem.at[3])
    out_e.start()

    for d in range(1, E):
        send_a(d).wait_send()
        send_w(d).wait_send()
        send_e(d).wait_send()
    for d in range(1, T):
        send_b(me, d, True).wait_send()
        send_m(d).wait_send()
        for k in range(1, E):
            send_b(epeer(k), d, False).wait_send()
    for j in range(T - 1):
        send_r(j).wait_send()
    for copy in (out_a, out_s, out_m, out_e):
        copy.wait()


def shards(
    mamba_input,
    mamba_gate,
    conv_state,
    scan_state,
    conv_weight,
    conv_bias,
    state_proj,
    step_proj,
    step_bias,
    decay_log,
    skip_gain,
    queries,
    new_entry,
    past_entries,
    lengths,
    expert_input,
    routes,
    slots,
    gates,
    inner_weights,
    outer_weights,
):
    E = lax.axis_size("expert")
    T = lax.axis_size("tensor")
    B, Dl = expert_input.shape
    L, _, F, D = inner_weights.shape
    S, H, HD = queries.shape
    C = mamba_input.shape[1]
    M = state_proj.shape[0]
    fc = min(F, 256)
    total_rows = E * L
    width = -(-total_rows // 128) * 128
    args = [
        mamba_input,
        mamba_gate,
        conv_state.transpose(1, 0, 2),
        scan_state,
        conv_weight,
        conv_bias.reshape(1, C),
        state_proj,
        step_proj,
        step_bias.reshape(1, C),
        decay_log,
        skip_gain.reshape(1, C),
        queries,
        new_entry,
        past_entries,
        lengths,
        expert_input,
        routes.T,
        gates.T,
        inner_weights,
        outer_weights,
    ]

    def held(a):
        return pltpu.VMEM(a.shape, a.dtype)

    outs = (
        jax.ShapeDtypeStruct((B, C), BF16),
        jax.ShapeDtypeStruct(scan_state.shape, F32),
        jax.ShapeDtypeStruct((S, H * HD), BF16),
        jax.ShapeDtypeStruct((B, Dl), BF16),
    )
    scratch = [held(a) for a in args[:14]] + [pltpu.SMEM(lengths.shape, jnp.int32), held(args[16]), held(args[17])]
    scratch += [held(inner_weights), pltpu.VMEM((T, L * F, Dl), BF16)]
    scratch += [
        pltpu.VMEM((E * B, D), BF16),
        pltpu.VMEM((E * B, width), F32),
        pltpu.VMEM((B, M), F32),
        pltpu.VMEM((T, B, M), F32),
        pltpu.VMEM((B, C), F32),
        pltpu.VMEM((B, C), F32),
        pltpu.VMEM((B, C), F32),
        pltpu.VMEM((B, C), F32),
        pltpu.VMEM((S, H, past_entries.shape[2]), F32),
        pltpu.VMEM((S, H, HD), F32),
        pltpu.VMEM((S, H, HD), F32),
        pltpu.VMEM((S, H * HD), BF16),
        pltpu.VMEM((B, C), BF16),
        pltpu.VMEM((E * B, L * F), BF16),
        pltpu.VMEM((T - 1, E * B, Dl), BF16),
        pltpu.VMEM((T, E * B, Dl), BF16),
        pltpu.VMEM((E * B, Dl), F32),
        pltpu.VMEM((E * B, Dl), BF16),
        pltpu.VMEM((E, B, Dl), BF16),
        pltpu.VMEM((B, Dl), BF16),
    ]
    sem = pltpu.SemaphoreType.DMA
    scratch += [sem((16,)), sem, sem((L, F // fc)), sem((T, L)), sem((4,)), sem]
    scratch += [sem((E,)), sem((E,)), sem((E,)), sem((E,)), sem((E, T)), sem((E, T)), sem((T,)), sem((T,))]
    scratch += [sem((T,)), sem((T,)), sem((E,)), sem((E,))]
    anywhere = pl.BlockSpec(memory_space=pl.ANY)
    mamba_out, next_state, attention_out, expert_out = pl.pallas_call(
        functools.partial(kernel, E, T, fc),
        out_shape=outs,
        in_specs=[anywhere] * len(args),
        out_specs=[anywhere] * len(outs),
        scratch_shapes=scratch,
        compiler_params=pltpu.CompilerParams(
            collective_id=0, has_side_effects=True, vmem_limit_bytes=67043328
        ),
    )(*args)
    return (mamba_out, next_state, attention_out, expert_out)


def solution(mesh):
    return jax.shard_map(
        shards,
        mesh=mesh,
        in_specs=(
            P(("parts", "expert"), "tensor"),
            P(("parts", "expert"), "tensor"),
            P(("parts", "expert"), None, "tensor"),
            P(("parts", "expert"), None, "tensor"),
            P(None, "tensor"),
            P("tensor"),
            P(None, "tensor"),
            P(None, "tensor"),
            P("tensor"),
            P(None, "tensor"),
            P("tensor"),
            P(("parts", "expert"), "tensor", None),
            P(("parts", "expert"), "tensor", None),
            P(("parts", "expert"), "tensor", None, None),
            P(("parts", "expert")),
            P(("parts", "expert"), "tensor"),
            P(("parts", "expert"), None),
            P(("parts", "expert"), None),
            P(("parts", "expert"), None),
            P("expert", None, "tensor", None),
            P("expert", "tensor", None),
        ),
        out_specs=(
            P(("parts", "expert"), "tensor"),
            P(("parts", "expert"), None, "tensor"),
            P(("parts", "expert"), "tensor"),
            P(("parts", "expert"), "tensor"),
        ),
        check_vma=False,
    )
```

```python
import functools

import jax
import jax.numpy as jnp
from jax import lax
from jax.experimental import pallas as pl
from jax.experimental.pallas import tpu as pltpu
from jax.sharding import PartitionSpec as P

EXPERTS = 8
MESH = pl.DeviceIdType.MESH
F32 = jnp.float32
BF16 = jnp.bfloat16
EXACT = lax.Precision.HIGHEST
NT = (((1,), (1,)), ((), ()))
NN = (((1,), (0,)), ((), ()))


def dot(a, b, dims):
    return lax.dot_general(a, b, dims, preferred_element_type=F32)


def eye(n):
    rows = lax.broadcasted_iota(jnp.int32, (n, n), 0)
    cols = lax.broadcasted_iota(jnp.int32, (n, n), 1)
    return jnp.where(rows == cols, 1.0, 0.0).astype(F32)


def kernel(
    E,
    T,
    fc,
    mi_h, mg_h, cs_h, ss_h, cw_h, cb_h, sp_h, tp_h, sb_h, dl_h, sg_h,
    q_h, ne_h, pe_h, len_h, xi_h, ro_h, ga_h, iw_h, ow_h,
    mo_h, ns_h, ao_h, eo_h,
    mi, mg, cs, ss, cw, cb, sp, tp, sb, dl, sg, q, ne, pe, lens, ro, ga, iw, ow,
    X, wr, mixp, mixr, conv, yv, stv, scuv, score, knew, vnew, ao, mo, hid, psend, rrecv, tot, tsend, erecv, eo,
    in_sem, pe_sem, iw_sem, ow_sem, out_sem, x_sem,
    as_sem, ar_sem, ws_sem, wr_sem, bs_sem, br_sem, ms_sem, mr_sem, rs_sem, rr_sem, es_sem, er_sem,
):
    me = lax.axis_index("expert")
    mt = lax.axis_index("tensor")
    B, Dl = xi_h.shape
    L, _, F, D = iw_h.shape
    S, H, HD = q_h.shape
    G = ne_h.shape[1]
    per = H // G
    N = dl_h.shape[0]
    R = tp_h.shape[0]
    reps = max(1, E // EXPERTS)
    nf = F // fc
    remote = functools.partial(pltpu.make_async_remote_copy, device_id_type=MESH)

    def epeer(d):
        return lax.rem(me + d, E)

    def tpeer(d):
        d = d % T
        if T & (T - 1):
            return lax.rem(mt + d, T)
        d = T - d if d else 0
        p = mt
        bit = 1
        while bit < T:
            if d & bit:
                p = p + bit - 2 * bit * lax.rem(p // bit, 2)
            bit *= 2
        return p

    barrier = pltpu.get_barrier_semaphore()
    for d in range(1, E):
        pl.semaphore_signal(barrier, inc=1, device_id={"expert": epeer(d)}, device_id_type=MESH)
    for d in range(1, T):
        pl.semaphore_signal(barrier, inc=1, device_id={"tensor": tpeer(d)}, device_id_type=MESH)

    pairs = [
        (ro_h, ro), (ga_h, ga), (len_h, lens), (cs_h, cs), (mi_h, mi), (cw_h, cw), (cb_h, cb), (sp_h, sp),
        (q_h, q), (ne_h, ne), (tp_h, tp), (sb_h, sb), (dl_h, dl), (sg_h, sg), (mg_h, mg), (ss_h, ss),
    ]
    local = {}
    for n, (src, dst) in enumerate(pairs):
        local[id(dst)] = pltpu.make_async_copy(src, dst, in_sem.at[n])

    def block(e, t):
        return X.at[pl.ds(pl.multiple_of(e * B, B), B), pl.ds(pl.multiple_of(t * Dl, Dl), Dl)]

    def rows(ref, e):
        return ref.at[pl.ds(pl.multiple_of(e * B, B), B)]

    own_x = pltpu.make_async_copy(xi_h, block(me, mt), x_sem)
    early = [ro, ga, lens, cs, mi, cw, cb, sp, q, ne]
    late = [tp, sb, dl, sg, mg, ss]
    for dst in early:
        local[id(dst)].start()
    own_x.start()
    pcopy = pltpu.make_async_copy(pe_h, pe, pe_sem)
    pcopy.start()
    for dst in late:
        local[id(dst)].start()

    def inner_copy(l, i):
        at = pl.ds(pl.multiple_of(i * fc, fc), fc)
        return pltpu.make_async_copy(iw_h.at[l, :, at, :], iw.at[l, :, at, :], iw_sem.at[l, i])

    for l in range(L):
        @pl.loop(0, nf)
        def _(i, l=l):
            inner_copy(l, i).start()

    def outer_copy(j, l):
        cols = pl.ds(pl.multiple_of(tpeer(j + 1) * Dl, Dl), Dl)
        return pltpu.make_async_copy(ow_h.at[l, :, cols], ow.at[j, pl.ds(l * F, F), :], ow_sem.at[j, l])

    for j in range(T):
        for l in range(L):
            outer_copy(j, l).start()

    local[id(ro)].wait()
    local[id(ga)].wait()
    width = wr.shape[1]
    table = jnp.zeros((width, B), F32)
    row_of = lax.broadcasted_iota(jnp.int32, (width, B), 0)
    for k in range(ro.shape[0]):
        first = ro[k : k + 1, :] * reps
        table = table + jnp.where((row_of >= first) & (row_of < first + reps), ga[k : k + 1, :], 0.0)
    table = lax.dot_general(eye(B), table, NT, precision=EXACT, preferred_element_type=F32)
    wr[pl.ds(pl.multiple_of(me * B, B), B), :] = table

    pl.semaphore_wait(barrier, E - 1 + T - 1)

    def send_a(d):
        p = epeer(d)
        return remote(src_ref=xi_h, dst_ref=block(me, mt), send_sem=as_sem.at[p], recv_sem=ar_sem.at[me],
                      device_id={"expert": p})

    def recv_a(e):
        return remote(src_ref=xi_h, dst_ref=block(e, mt), send_sem=as_sem.at[e], recv_sem=ar_sem.at[e],
                      device_id={"expert": e})

    def send_w(d):
        p = epeer(d)
        return remote(src_ref=rows(wr, me), dst_ref=rows(wr, me), send_sem=ws_sem.at[p], recv_sem=wr_sem.at[me],
                      device_id={"expert": p})

    def recv_w(e):
        return remote(src_ref=rows(wr, e), dst_ref=rows(wr, e), send_sem=ws_sem.at[e], recv_sem=wr_sem.at[e],
                      device_id={"expert": e})

    def send_b(e, d, own):
        p = tpeer(d)
        return remote(src_ref=xi_h if own else block(e, mt), dst_ref=block(e, mt), send_sem=bs_sem.at[e, p],
                      recv_sem=br_sem.at[e, mt], device_id={"tensor": p})

    def recv_b(e, t):
        return remote(src_ref=xi_h, dst_ref=block(e, t), send_sem=bs_sem.at[e, t], recv_sem=br_sem.at[e, t],
                      device_id={"tensor": t})

    for d in range(1, E):
        send_a(d).start()
    for d in range(1, T):
        send_b(me, d, True).start()
    for d in range(1, E):
        send_w(d).start()

    for ref in (cs, mi, cw, cb, sp):
        local[id(ref)].wait()
    taps = cw.shape[0]
    pre = mi[...].astype(F32) * cw[taps - 1 : taps, :]
    for k in range(taps - 1):
        pre = pre + cs[k].astype(F32) * cw[k : k + 1, :]
    act = jax.nn.silu(pre + cb[...])
    conv[...] = act
    mixp[...] = dot(act.astype(BF16), sp[...], NT)

    def send_m(d):
        p = tpeer(d)
        return remote(src_ref=mixp, dst_ref=mixr.at[mt], send_sem=ms_sem.at[p], recv_sem=mr_sem.at[mt],
                      device_id={"tensor": p})

    def recv_m(t):
        return remote(src_ref=mixp, dst_ref=mixr.at[t], send_sem=ms_sem.at[t], recv_sem=mr_sem.at[t],
                      device_id={"tensor": t})

    for d in range(1, T):
        send_m(d).start()

    head_row = lax.broadcasted_iota(jnp.int32, (H, HD), 0)
    places = lax.broadcasted_iota(jnp.int32, (H, pe.shape[2]), 1)
    place_row = lax.broadcasted_iota(jnp.int32, (H, pe.shape[2]), 0)

    def by_group(parts, row):
        out = parts[0]
        for g in range(1, G):
            out = jnp.where(row >= g * per, parts[g], out)
        return out

    def attention_scores():
        for ref in (lens, q, ne):
            local[id(ref)].wait()
        pcopy.wait()
        for s in range(S):
            qs = q[s]
            sc = by_group([dot(qs, pe[s, g, :, :HD], NT) for g in range(G)], place_row)
            score[s] = jnp.where(places < lens[s], sc, -jnp.inf)
            entry = ne[s].astype(F32)
            knew[s] = by_group([jnp.broadcast_to(entry[g : g + 1, :HD], (H, HD)) for g in range(G)], head_row)
            vnew[s] = by_group([jnp.broadcast_to(entry[g : g + 1, HD:], (H, HD)) for g in range(G)], head_row)

    def forward():
        for d in range(1, E):
            e = epeer(d)
            recv_a(e).wait_recv()
            for k in range(1, T):
                send_b(e, k, False).start()

    def attention_rest():
        scaling = HD ** (-0.5)
        sc = score[...] * scaling
        own_score = jnp.sum(q[...].astype(F32) * knew[...], axis=2, keepdims=True) * scaling
        highest = jnp.maximum(jnp.max(sc, axis=2, keepdims=True), own_score)
        weights = jnp.exp(sc - highest)
        own_weight = jnp.exp(own_score - highest)
        total = jnp.sum(weights, axis=2, keepdims=True) + own_weight
        score[...] = weights / total
        vnew[...] = (own_weight / total).astype(BF16).astype(F32) * vnew[...]
        for s in range(S):
            low = score[s].astype(BF16)
            mixed = by_group([dot(low, pe[s, g, :, HD:], NN) for g in range(G)], head_row)
            knew[s] = mixed + vnew[s]
        for h in range(H):
            ao[:, h * HD : (h + 1) * HD] = knew[:, h, :].astype(BF16)
        out_a = pltpu.make_async_copy(ao, ao_h, out_sem.at[0])
        out_a.start()
        return out_a

    def mamba():
        for ref in (tp, sb, dl, sg, mg, ss):
            local[id(ref)].wait()
        mixing = mixp[...]
        for d in range(1, T):
            t = tpeer(d)
            recv_m(t).wait_recv()
            mixing = mixing + mixr[t]
        step = jax.nn.softplus(dot(mixing[:, :R].astype(BF16), tp[...], NN) + sb[...])
        stv[...] = step
        scuv[...] = step * conv[...]
        coef = lax.dot_general(mixing[:, R:], eye(S), (((0,), (0,)), ((), ())), precision=EXACT, preferred_element_type=F32)
        decay = jnp.exp(dl[...])
        for s in range(S):
            nxt = jnp.exp(-stv[s : s + 1, :] * decay) * ss[s] + scuv[s : s + 1, :] * coef[:N, s : s + 1]
            ss[s] = nxt
            yv[s : s + 1, :] = jnp.sum(nxt * coef[N:, s : s + 1], axis=0, keepdims=True)
        out_s = pltpu.make_async_copy(ss, ns_h, out_sem.at[1])
        out_s.start()
        mo[...] = ((yv[...] + sg[...] * conv[...]) * jax.nn.silu(mg[...].astype(F32))).astype(BF16)
        out_m = pltpu.make_async_copy(mo, mo_h, out_sem.at[2])
        out_m.start()
        return (out_s, out_m)

    forward()
    attention_scores()
    out_a = attention_rest()
    own_x.wait()
    for d in range(1, E):
        recv_w(epeer(d)).wait_recv()
    for e in range(E):
        for d in range(1, T):
            recv_b(lax.rem(me + e, E), tpeer(d)).wait_recv()
    lanes = lax.broadcasted_iota(jnp.int32, wr.shape, 1)
    for l in range(L):
        weight = jnp.sum(jnp.where(lanes == me * L + l, wr[...], 0.0), axis=1, keepdims=True)

        @pl.loop(0, nf)
        def _(i, l=l, weight=weight):
            inner_copy(l, i).wait()
            at = pl.ds(pl.multiple_of(i * fc, fc), fc)
            x = X[...]
            gate = dot(x, iw[l, 0, at, :], NT)
            up = dot(x, iw[l, 1, at, :], NT)
            to = pl.ds(pl.multiple_of(l * F + i * fc, fc), fc)
            hid[:, to] = (jax.nn.silu(gate) * up * weight).astype(BF16)

    def send_r(j):
        p = tpeer(j + 1)
        return remote(src_ref=psend.at[j], dst_ref=rrecv.at[mt], send_sem=rs_sem.at[j], recv_sem=rr_sem.at[mt],
                      device_id={"tensor": p})

    def recv_r(t):
        return remote(src_ref=psend.at[0], dst_ref=rrecv.at[t], send_sem=rs_sem.at[0], recv_sem=rr_sem.at[t],
                      device_id={"tensor": t})

    for j in range(T):
        for l in range(L):
            outer_copy(j, l).wait()
        part = dot(hid[...], ow[j], NN)
        if j < T - 1:
            psend[j] = part.astype(BF16)
            send_r(j).start()
    for d in range(1, T):
        t = tpeer(d)
        recv_r(t).wait_recv()
        part = part + rrecv[t].astype(F32)
    tot[...] = part
    tsend[...] = part.astype(BF16)

    def send_e(d):
        p = epeer(d)
        return remote(src_ref=rows(tsend, p), dst_ref=erecv.at[me], send_sem=es_sem.at[p], recv_sem=er_sem.at[me],
                      device_id={"expert": p})

    def recv_e(e):
        return remote(src_ref=rows(tsend, e), dst_ref=erecv.at[e], send_sem=es_sem.at[e], recv_sem=er_sem.at[e],
                      device_id={"expert": e})

    for d in range(1, E):
        send_e(d).start()
    out_s, out_m = mamba()
    final = tot[pl.ds(pl.multiple_of(me * B, B), B), :]
    for d in range(1, E):
        e = epeer(d)
        recv_e(e).wait_recv()
        final = final + erecv[e].astype(F32)
    eo[...] = final.astype(BF16)
    out_e = pltpu.make_async_copy(eo, eo_h, out_sem.at[3])
    out_e.start()

    for d in range(1, E):
        send_a(d).wait_send()
        send_w(d).wait_send()
        send_e(d).wait_send()
    for d in range(1, T):
        send_b(me, d, True).wait_send()
        send_m(d).wait_send()
        for k in range(1, E):
            send_b(epeer(k), d, False).wait_send()
    for j in range(T - 1):
        send_r(j).wait_send()
    for copy in (out_a, out_s, out_m, out_e):
        copy.wait()


def hand_over(*refs):
    count = (len(refs) - 2) // 3
    sources, results, held = refs[:count], refs[count : 2 * count], refs[2 * count : 3 * count]
    in_sem, out_sem = refs[3 * count :]
    steps = []
    for n in range(count):
        pieces = 4 if len(sources[n].shape) == 3 else 1
        size = sources[n].shape[0] // pieces
        for k in range(pieces):
            at = pl.ds(k * size, size)
            slot = len(steps)
            steps.append((
                pltpu.make_async_copy(sources[n].at[at], held[n].at[at], in_sem.at[slot]),
                pltpu.make_async_copy(held[n].at[at], results[n].at[at], out_sem.at[slot]),
            ))
    for fetch, _ in steps:
        fetch.start()
    for fetch, put in steps:
        fetch.wait()
        put.start()
    for _, put in steps:
        put.wait()


def shards(
    mamba_input,
    mamba_gate,
    conv_state,
    scan_state,
    conv_weight,
    conv_bias,
    state_proj,
    step_proj,
    step_bias,
    decay_log,
    skip_gain,
    queries,
    new_entry,
    past_entries,
    lengths,
    expert_input,
    routes,
    slots,
    gates,
    inner_weights,
    outer_weights,
):
    E = lax.axis_size("expert")
    T = lax.axis_size("tensor")
    B, Dl = expert_input.shape
    L, _, F, D = inner_weights.shape
    S, H, HD = queries.shape
    C = mamba_input.shape[1]
    M = state_proj.shape[0]
    fc = min(F, 1024)
    total_rows = E * L
    width = -(-total_rows // 128) * 128
    args = [
        mamba_input,
        mamba_gate,
        conv_state.transpose(1, 0, 2),
        scan_state,
        conv_weight,
        conv_bias.reshape(1, C),
        state_proj,
        step_proj,
        step_bias.reshape(1, C),
        decay_log,
        skip_gain.reshape(1, C),
        queries,
        new_entry,
        past_entries,
        lengths,
        expert_input,
        routes.T,
        gates.T,
        inner_weights,
        outer_weights,
    ]

    def held(a):
        return pltpu.VMEM(a.shape, a.dtype)

    outs = (
        jax.ShapeDtypeStruct((B, C), BF16),
        jax.ShapeDtypeStruct(scan_state.shape, F32),
        jax.ShapeDtypeStruct((S, H * HD), BF16),
        jax.ShapeDtypeStruct((B, Dl), BF16),
    )
    scratch = [held(a) for a in args[:14]] + [pltpu.SMEM(lengths.shape, jnp.int32), held(args[16]), held(args[17])]
    scratch += [held(inner_weights), pltpu.VMEM((T, L * F, Dl), BF16)]
    scratch += [
        pltpu.VMEM((E * B, D), BF16),
        pltpu.VMEM((E * B, width), F32),
        pltpu.VMEM((B, M), F32),
        pltpu.VMEM((T, B, M), F32),
        pltpu.VMEM((B, C), F32),
        pltpu.VMEM((B, C), F32),
        pltpu.VMEM((B, C), F32),
        pltpu.VMEM((B, C), F32),
        pltpu.VMEM((S, H, past_entries.shape[2]), F32),
        pltpu.VMEM((S, H, HD), F32),
        pltpu.VMEM((S, H, HD), F32),
        pltpu.VMEM((S, H * HD), BF16),
        pltpu.VMEM((B, C), BF16),
        pltpu.VMEM((E * B, L * F), BF16),
        pltpu.VMEM((T - 1, E * B, Dl), BF16),
        pltpu.VMEM((T, E * B, Dl), BF16),
        pltpu.VMEM((E * B, Dl), F32),
        pltpu.VMEM((E * B, Dl), BF16),
        pltpu.VMEM((E, B, Dl), BF16),
        pltpu.VMEM((B, Dl), BF16),
    ]
    sem = pltpu.SemaphoreType.DMA
    scratch += [sem((16,)), sem, sem((L, F // fc)), sem((T, L)), sem((4,)), sem]
    scratch += [sem((E,)), sem((E,)), sem((E,)), sem((E,)), sem((E, T)), sem((E, T)), sem((T,)), sem((T,))]
    scratch += [sem((T,)), sem((T,)), sem((E,)), sem((E,))]
    anywhere = pl.BlockSpec(memory_space=pl.ANY)
    mamba_out, next_state, attention_out, expert_out = pl.pallas_call(
        functools.partial(kernel, E, T, fc),
        out_shape=outs,
        in_specs=[anywhere] * len(args),
        out_specs=[anywhere] * len(outs),
        scratch_shapes=scratch,
        compiler_params=pltpu.CompilerParams(
            collective_id=0, has_side_effects=True, vmem_limit_bytes=67043328
        ),
    )(*args)
    results = (next_state, mamba_out, attention_out, expert_out)
    next_state, mamba_out, attention_out, expert_out = pl.pallas_call(
        hand_over,
        out_shape=tuple(jax.ShapeDtypeStruct(a.shape, a.dtype) for a in results),
        in_specs=[anywhere] * len(results),
        out_specs=[anywhere] * len(results),
        scratch_shapes=[held(a) for a in results] + [sem((8,)), sem((8,))],
    )(*results)
    return (mamba_out, next_state, attention_out, expert_out)


def solution(mesh):
    return jax.shard_map(
        shards,
        mesh=mesh,
        in_specs=(
            P(("parts", "expert"), "tensor"),
            P(("parts", "expert"), "tensor"),
            P(("parts", "expert"), None, "tensor"),
            P(("parts", "expert"), None, "tensor"),
            P(None, "tensor"),
            P("tensor"),
            P(None, "tensor"),
            P(None, "tensor"),
            P("tensor"),
            P(None, "tensor"),
            P("tensor"),
            P(("parts", "expert"), "tensor", None),
            P(("parts", "expert"), "tensor", None),
            P(("parts", "expert"), "tensor", None, None),
            P(("parts", "expert")),
            P(("parts", "expert"), "tensor"),
            P(("parts", "expert"), None),
            P(("parts", "expert"), None),
            P(("parts", "expert"), None),
            P("expert", None, "tensor", None),
            P("expert", "tensor", None),
        ),
        out_specs=(
            P(("parts", "expert"), "tensor"),
            P(("parts", "expert"), None, "tensor"),
            P(("parts", "expert"), "tensor"),
            P(("parts", "expert"), "tensor"),
        ),
        check_vma=False,
    )
```
